32 devices in a mesh: dp: 2 (over core), context: 4 (over y, x), expert: 4 (over z).
Axes of the slice: x: 2, y: 2, z: 4, core: 2. Of those that a mesh axis runs over, the one named last changes fastest.
Arguments:
- inputs: bfloat16 [2, 4096, 2048], P('dp', ('context', 'expert')), may hold values from -6 to 6
- cotangent: bfloat16 [2, 4096, 2048], P('dp', ('context', 'expert')), may hold values from -6 to 6
- stretch_ids: int32 [8], replicated, may hold values from 0 to 7, as said below
- expert_ids: int32 [2, 4096, 8], P('dp', ('context', 'expert')), may hold values from 0 to 15, all different within a row; in each aligned block of 256 rows (0 to 255, 256 to 511, ..., all dimensions but the last counted through in order) at most 192 rows name the same one
- attn_gain: float32 [2048], replicated, may hold values from 0.5 to 1.5
- query_gain: float32 [128], replicated, may hold values from 0.5 to 2
- key_gain: float32 [128], replicated, may hold values from 0.5 to 2
- w_query: bfloat16 [2048, 4096], P(None, 'expert'), may hold values from -0.125 to 0.125
- key_matrix: bfloat16 [2048, 512], replicated, may hold values from -0.125 to 0.125
- value_matrix: bfloat16 [2048, 512], replicated, may hold values from -0.125 to 0.125
- w_out: bfloat16 [4096, 2048], P('expert'), may hold values from -0.375 to 0.375
- mlp_gain: float32 [2048], replicated, may hold values from 0.5 to 1.5
- w_router: bfloat16 [2048, 16], replicated, may hold values from -0.125 to 0.125
- w_gate: bfloat16 [16, 2048, 768], P(('context', 'expert')), may hold values from -0.125 to 0.125
- w_up: bfloat16 [16, 2048, 768], P(('context', 'expert')), may hold values from -0.125 to 0.125
- w_down: bfloat16 [16, 768, 2048], P(('context', 'expert')), may hold values from -0.21875 to 0.21875
Outputs:
- output: bfloat16 [2, 4096, 2048], P('dp', ('context', 'expert'))
- grad_inputs: float32 [2, 4096, 2048], P('dp', ('context', 'expert'))
- grad_attn_gain: float32 [2048], replicated
- grad_query_gain: float32 [128], replicated
- grad_key_gain: float32 [128], replicated
- grad_w_query: float32 [2048, 4096], P(None, 'expert')
- grad_w_key: float32 [2048, 512], replicated
- grad_w_value: float32 [2048, 512], replicated
- grad_w_out: float32 [4096, 2048], P('expert')
- grad_mlp_gain: float32 [2048], replicated
- grad_w_router: float32 [2048, 16], replicated
- grad_w_gate: float32 [16, 2048, 768], P(('context', 'expert'), 'dp')
- grad_w_up: float32 [16, 2048, 768], P(('context', 'expert'), 'dp')
- grad_w_down: float32 [16, 768, 2048], P(('context', 'expert'), None, 'dp')
The draws below stay inside these ranges and needn't reach their ends.
Inputs may be any that keep to these rules, and one draw needn't show every extreme that they name: `stretch_ids`: entries 2 r and 2 r + 1 are k and 7 - k for some k, and each block number appears once. `expert_ids`: a token names 8 different experts; among the tokens of one device no expert is named more than 192 times, a bound that some block reaches.
All inputs are finite; a program needn't handle non-finite values.
Results may differ from the reference program's by a relative error of at most 0.019.
Values may be sent and summed in bfloat16 or wider, within the bound.
No kernel may reach another device: no remote copies, remote signals or barrier semaphores. Data moves between devices by JAX's collectives and lax.ppermute only.
A program may use at most 320 MiB of HBM per device.

```python
import math
import jax
import jax.numpy as jnp
import numpy as np
from jax import lax

MODEL_WIDTH = 2048
QUERY_HEADS = 32
KEY_VALUE_HEADS = 4
HEAD_SIZE = 128
EXP_FF = 768
TOPK = 8
HALF = 512
STRETCHES = 8
SEQUENCE_TOKENS = 4096
TOK_DEV = 256
EXPERTS = 16
CAP = 192
N_DP = 2


def draw_stretch_ids(key, part):
    order = jax.random.permutation(key, STRETCHES // 2).astype(jnp.int32)
    paired = jnp.stack([order, STRETCHES - 1 - order], axis=1)
    return paired.reshape(STRETCHES).astype(jnp.int32)


def gain_draw(key):
    spread = jax.random.uniform(key, (HEAD_SIZE,), jnp.float32, math.log(0.5), math.log(2.0))
    return jnp.exp(spread)


def draw_query_gain(key, part):
    return gain_draw(jax.random.fold_in(key, 11))


def draw_key_gain(key, part):
    return gain_draw(jax.random.fold_in(key, 23))


def level_of(key, extent, pieces, least, top_value):
    gain = 1.0
    for axis_at, shards_of in pieces:
        draws = jax.random.uniform(jax.random.fold_in(jax.random.fold_in(key, 6), axis_at), (shards_of,), jnp.float32, least / len(pieces), top_value / len(pieces))
        gain = gain * jnp.repeat(jnp.exp(draws), extent[axis_at] // shards_of).reshape((-1,) + (1,) * (len(extent) - 1 - axis_at))
    return gain


def routed_block(own_key, own, number, rows, count, top, reach, slope):
    ranking = jax.random.permutation(own_key, count)
    heavy_load, common = load_shares(count, rows * top, reach, slope, True), load_shares(count, rows * top, reach, slope, False)
    places = jnp.arange(count)

    def named(sizes, rotation):
        used = int((sizes > 0).sum())
        fixed = max(1, used // 4)
        moved = fixed + (places - fixed + rotation * (used - fixed)) % max(1, count - fixed)
        return jnp.zeros((count,), jnp.int32).at[ranking[jnp.where(places < fixed, places, moved)]].set(jnp.asarray(sizes, jnp.int32))

    sizes = jnp.where(number % 4 == 0, named(heavy_load, number // 4), named(common, number - number // 4 - 1))
    mixed = jax.random.permutation(jax.random.fold_in(own, 3), count)
    donor, sink = mixed[0:count // 2 * 2:2], mixed[1:count // 2 * 2:2]
    room = jnp.minimum(sizes[donor] - 1, reach - sizes[sink]) // 2
    room = jnp.where((donor == ranking[0]) | (sink == ranking[0]) | (sizes[sink] == 0), 0, jnp.maximum(room, 0))
    moved = jax.random.randint(jax.random.fold_in(own, 4), (count // 2,), 0, 1 << 20) % (room + 1)
    sizes = sizes.at[donor].add(-moved).at[sink].add(moved)
    members = jnp.searchsorted(jnp.cumsum(sizes), jnp.arange(rows * top), side="right").astype(jnp.int32)
    table = members.reshape(top, rows).T
    table = table[jax.random.permutation(jax.random.fold_in(own, 1), rows)]
    rotation = jax.random.randint(jax.random.fold_in(own, 2), (rows, 1), 0, top)
    return jnp.take_along_axis(table, (jnp.arange(top)[None, :] + rotation) % top, axis=1)


def load_shares(amount, total, reach, skew, full):
    portions = [(1 << 20) // math.isqrt(rank ** skew) + 1 for rank in range(1, amount + 1)]
    largest = reach if full else min(reach, max(-(-total // amount), total * portions[0] // sum(portions)))
    least = 1 if total - largest >= amount - 1 else 0
    given, spare = [largest] + [least] * (amount - 1), total - largest - least * (amount - 1)
    while spare > 0:
        free = [i for i in range(1, amount) if given[i] < largest] or [i for i in range(1, amount) if given[i] < reach]
        pool, budget = sum([portions[i] for i in free]), spare
        for i in free:
            extra = min(reach - given[i], max(1, budget * portions[i] // pool), spare)
            given[i] = given[i] + extra
            spare = spare - extra
    return np.array(given)


def scatter_about(own_key, shape, deviation, reach, shards=(), kind=jnp.bfloat16):
    gain = level_of(own_key, shape, shards, -0.22, 0.18) if shards else 1.0
    result = jax.random.normal(own_key, shape, jnp.float32) * deviation * gain
    return jnp.minimum(jnp.maximum(result, -reach), reach).astype(kind)


def setup_inputs(seed: int = 0) -> dict:
    key_of = jax.random.split(jax.random.key(seed), 17)
    inputs = scatter_about(key_of[0], (N_DP, SEQUENCE_TOKENS, MODEL_WIDTH), 1.0, 6.0, ((0, 2), (1, 16)))
    cotangent = scatter_about(key_of[1], (N_DP, SEQUENCE_TOKENS, MODEL_WIDTH), 1.0, 6.0, ((0, 2), (1, 16)))
    stretch_ids = draw_stretch_ids(jax.random.fold_in(key_of[16], 71), 0)
    expert_ids_keys = jax.random.split(jax.random.fold_in(key_of[3], 1), N_DP * SEQUENCE_TOKENS // TOK_DEV)
    expert_ids_turns = jax.random.permutation(jax.random.fold_in(key_of[3], 3), N_DP * SEQUENCE_TOKENS // TOK_DEV)
    expert_ids = jax.vmap(lambda own, number: routed_block(jax.random.fold_in(key_of[3], 2), own, number, TOK_DEV, EXPERTS, TOPK, CAP, 1))(expert_ids_keys, expert_ids_turns).reshape((N_DP, SEQUENCE_TOKENS, TOPK))
    attn_gain = jnp.clip(1.0 + 0.1 * jax.random.normal(key_of[4], (MODEL_WIDTH,), jnp.float32), 0.5, 1.5)
    query_gain = draw_query_gain(jax.random.fold_in(key_of[16], 71), 0)
    key_gain = draw_key_gain(jax.random.fold_in(key_of[16], 71), 0)
    w_query = scatter_about(key_of[7], (MODEL_WIDTH, QUERY_HEADS * HEAD_SIZE), MODEL_WIDTH ** -0.5, 0.125, ((1, 4),))
    key_matrix = scatter_about(key_of[8], (MODEL_WIDTH, KEY_VALUE_HEADS * HEAD_SIZE), MODEL_WIDTH ** -0.5, 0.125)
    value_matrix = scatter_about(key_of[9], (MODEL_WIDTH, KEY_VALUE_HEADS * HEAD_SIZE), MODEL_WIDTH ** -0.5, 0.125)
    w_out = scatter_about(key_of[10], (QUERY_HEADS * HEAD_SIZE, MODEL_WIDTH), (QUERY_HEADS * HEAD_SIZE // 16) ** -0.5, 0.375, ((0, 4),))
    mlp_gain = jnp.clip(1.0 + 0.1 * jax.random.normal(key_of[11], (MODEL_WIDTH,), jnp.float32), 0.5, 1.5)
    w_router = scatter_about(key_of[12], (MODEL_WIDTH, EXPERTS), MODEL_WIDTH ** -0.5, 0.125)
    w_gate = scatter_about(key_of[13], (EXPERTS, MODEL_WIDTH, EXP_FF), MODEL_WIDTH ** -0.5, 0.125, ((0, 16),))
    w_up = scatter_about(key_of[14], (EXPERTS, MODEL_WIDTH, EXP_FF), MODEL_WIDTH ** -0.5, 0.125, ((0, 16),))
    w_down = scatter_about(key_of[15], (EXPERTS, EXP_FF, MODEL_WIDTH), EXP_FF ** -0.5, 0.21875, ((0, 16),))
    return dict(inputs=inputs, cotangent=cotangent, stretch_ids=stretch_ids, expert_ids=expert_ids, attn_gain=attn_gain, query_gain=query_gain, key_gain=key_gain, w_query=w_query, key_matrix=key_matrix, value_matrix=value_matrix, w_out=w_out, mlp_gain=mlp_gain, w_router=w_router, w_gate=w_gate, w_up=w_up, w_down=w_down)


epsilon = 1e-06
rope_base = 1000000.0
masked_score = -1e+30
highest = lax.Precision.HIGHEST

@jax.custom_vjp
def low(v):
    return lax.optimization_barrier(v.astype(jnp.bfloat16)).astype(jnp.float32)

@jax.custom_vjp
def low_back(v):
    return v

def low_keep(v):
    return (low(v), None)

def low_pass(kept, grad):
    return (grad,)

def back_keep(v):
    return (v, None)

def back_low(kept, grad):
    return (low(grad),)
low.defvjp(low_keep, low_pass)
low_back.defvjp(back_keep, back_low)

def matrix_product(left, right):
    return jnp.dot(left, right, precision=highest)

def apply_norm(matrix, norm_gain):
    inv_rms = lax.rsqrt(lax.optimization_barrier(jnp.mean(matrix * matrix, axis=-1, keepdims=True)) + epsilon)
    return matrix * inv_rms * norm_gain

def rotate_pairs(matrix, positions):
    half_dim = matrix.shape[-1] // 2
    frequency = jnp.exp(jnp.arange(half_dim, dtype=jnp.float32) * (-2.0 * math.log(rope_base) / matrix.shape[-1]))
    angles = positions.astype(jnp.float32)[:, None] * frequency[None, :]
    cosine = jnp.cos(angles)[:, None, :]
    sine_part = jnp.sin(angles)[:, None, :]
    front_half = matrix[..., :half_dim]
    back_half = matrix[..., half_dim:]
    return jnp.concatenate([front_half * cosine - back_half * sine_part, back_half * cosine + front_half * sine_part], axis=-1)

def one_sequence(tokens, routes, positions, params):
    attn_gain, query_gain, key_gain, w_query, key_matrix, value_matrix, w_out, mlp_gain, w_router, w_gate, w_up, w_down = params
    normalized_rows = low(apply_norm(tokens, attn_gain))
    query_proj = low_back(matrix_product(normalized_rows, w_query)).reshape(SEQUENCE_TOKENS, QUERY_HEADS, HEAD_SIZE)
    queries = low(rotate_pairs(apply_norm(query_proj, query_gain), positions))
    key_projected = low_back(matrix_product(normalized_rows, key_matrix)).reshape(SEQUENCE_TOKENS, KEY_VALUE_HEADS, HEAD_SIZE)
    keys = low(rotate_pairs(apply_norm(key_projected, key_gain), positions))
    value_rows = low_back(low(matrix_product(normalized_rows, value_matrix))).reshape(SEQUENCE_TOKENS, KEY_VALUE_HEADS, HEAD_SIZE)
    group_width = QUERY_HEADS // KEY_VALUE_HEADS
    block_len = min(512, SEQUENCE_TOKENS)
    score_scale = 1.0 / math.sqrt(HEAD_SIZE)
    block_positions_all = positions.reshape(SEQUENCE_TOKENS // block_len, block_len)

    def one_head(head_args):
        head_queries, head_keys, head_values = head_args

        def one_block(block_args):
            block_queries, block_positions = block_args
            raw_scores = matrix_product(block_queries, head_keys.T)
            scores = low_back(raw_scores * score_scale)
            scores = jnp.where(positions[None, :] <= block_positions[:, None], scores, masked_score)
            log_total = jax.nn.logsumexp(scores, axis=1, keepdims=True)
            weights_soft = jnp.exp(scores - log_total)
            return matrix_product(low(weights_soft), head_values)
        blocks = lax.map(jax.checkpoint(one_block), (head_queries.reshape(SEQUENCE_TOKENS // block_len, block_len, HEAD_SIZE), block_positions_all))
        return blocks.reshape(SEQUENCE_TOKENS, HEAD_SIZE)
    heads_out = lax.map(one_head, (queries.transpose(1, 0, 2), jnp.repeat(keys, group_width, axis=1).transpose(1, 0, 2), jnp.repeat(value_rows, group_width, axis=1).transpose(1, 0, 2)))
    attn_mix = low_back(low(heads_out.transpose(1, 0, 2).reshape(SEQUENCE_TOKENS, QUERY_HEADS * HEAD_SIZE)))
    branch = low_back(matrix_product(attn_mix, w_out))
    middle = tokens + branch
    hidden = low(apply_norm(middle, mlp_gain))
    logits = low_back(matrix_product(hidden, w_router))
    chosen = jnp.take_along_axis(logits, routes, axis=1)
    gate_probs = jax.nn.softmax(chosen, axis=-1)

    def expert_step(mixture, item):
        gate_mat, up_mat, down_mat, number = item
        weighting = lax.optimization_barrier(jnp.sum(jnp.where(routes == number, gate_probs, 0.0), axis=1))
        expert_in = low_back(hidden)
        gate_pre = low_back(matrix_product(expert_in, gate_mat))
        up_pre = low_back(matrix_product(expert_in, up_mat))
        active = low(jax.nn.silu(gate_pre) * up_pre)
        expert_out = low_back(low(matrix_product(active, down_mat)))
        return (mixture + weighting[:, None] * expert_out, None)
    start_mix = jnp.zeros((SEQUENCE_TOKENS, MODEL_WIDTH), jnp.float32)
    mixture, unused = lax.scan(jax.checkpoint(expert_step), start_mix, (w_gate, w_up, w_down, jnp.arange(EXPERTS, dtype=jnp.int32)))
    return middle + mixture

def reference(inputs, cotangent, stretch_ids, expert_ids, attn_gain, query_gain, key_gain, w_query, key_matrix, value_matrix, w_out, mlp_gain, w_router, w_gate, w_up, w_down):
    offsets = jnp.arange(HALF, dtype=jnp.int32)
    positions = (stretch_ids[:, None] * HALF + offsets[None, :]).reshape(SEQUENCE_TOKENS).astype(jnp.int32)
    params = jax.tree.map(lambda value: value.astype(jnp.float32), (attn_gain, query_gain, key_gain, w_query, key_matrix, value_matrix, w_out, mlp_gain, w_router, w_gate, w_up, w_down))

    def forward(tokens_all, weights_all):
        results = [one_sequence(tokens_all[seq_index], expert_ids[seq_index], positions, weights_all) for seq_index in range(N_DP)]
        return jnp.stack(results)
    output, pullback = jax.vjp(forward, inputs.astype(jnp.float32), params)
    grad_inputs, grad_params = pullback(cotangent.astype(jnp.float32))
    grad_attn_gain, grad_query_gain, grad_key_gain, grad_w_query, grad_w_key, grad_w_value, grad_w_out, grad_mlp_gain, grad_w_router, grad_w_gate, grad_w_up, grad_w_down = grad_params
    return (output.astype(jnp.bfloat16), grad_inputs, grad_attn_gain, grad_query_gain, grad_key_gain, grad_w_query, grad_w_key, grad_w_value, grad_w_out, grad_mlp_gain, grad_w_router, grad_w_gate, grad_w_up, grad_w_down)
```

```python
import functools
import math

import jax
import jax.numpy as jnp
from jax import lax
from jax.experimental import pallas as pl
from jax.experimental.pallas import tpu as pltpu
from jax.sharding import PartitionSpec as P

QUERY_HEADS = 32
KEY_VALUE_HEADS = 4
HALF = 512
HEAD = 128


epsilon = 1e-06
rope_base = 1000000.0
low = jnp.bfloat16
wide = jnp.float32

NT = (((1,), (1,)), ((), ()))
TN = (((0,), (0,)), ((), ()))
NN = (((1,), (0,)), ((), ()))


def mm(a, b, dims):
    return lax.dot_general(a, b, dims, preferred_element_type=wide)


def attn_fwd_body(scale2, heads, unroll, tab, q_ref, kv_ref, o_ref, lg_ref, acc):
    step = pl.program_id(0)
    q_row = pl.multiple_of(tab[0, step] * HALF, HALF)
    k_row = pl.multiple_of(tab[1, step] * HALF, HALF)
    diag, first = tab[2, step], tab[3, step]

    @pl.when(first == 1)
    def _():
        acc[...] = jnp.zeros_like(acc)

    def run(masked):
        keys = kv_ref[pl.ds(k_row, HALF), :HEAD]
        vals = kv_ref[pl.ds(k_row, HALF), HEAD:]
        vals = jnp.concatenate([vals, jnp.ones_like(vals)], axis=1)

        def one(head):
            cols = pl.ds(pl.multiple_of(head * HEAD, HEAD), HEAD)
            s = mm(q_ref[pl.ds(q_row, HALF), cols], keys, NT)
            p = jnp.exp2(s * scale2)
            if masked:
                rows = lax.broadcasted_iota(jnp.int32, p.shape, 0)
                p = jnp.where(lax.broadcasted_iota(jnp.int32, p.shape, 1) <= rows, p, 0.0)
            acc[head] += mm(p.astype(low), vals, NN)

        def body(i, c):
            for u in range(unroll):
                one(i * unroll + u)
            return c

        lax.fori_loop(0, heads // unroll, body, 0)

    @pl.when(diag == 0)
    def _():
        run(False)

    @pl.when(diag == 1)
    def _():
        run(True)

        def fin(head, c):
            cols = pl.ds(pl.multiple_of(head * HEAD, HEAD), HEAD)
            a = acc[head]
            total = a[:, HEAD:]
            o_ref[pl.ds(q_row, HALF), cols] = (a[:, :HEAD] / total).astype(low)
            lg_ref[pl.ds(head, 1), pl.ds(q_row, HALF)] = jnp.log2(total.T[:1, :])
            return c

        lax.fori_loop(0, heads, fin, 0)


def attn_bwd_body(scale2, heads, unroll, tab, q_ref, kv_ref, o_ref, lg_ref, do_ref, dq_ref, dkv_ref, dk, dv, delta):
    step = pl.program_id(0)
    q_row = pl.multiple_of(tab[0, step] * HALF, HALF)
    k_row = pl.multiple_of(tab[1, step] * HALF, HALF)
    diag, first = tab[2, step], tab[3, step]

    @pl.when(step == 0)
    def _():
        dk[...] = jnp.zeros_like(dk)
        dv[...] = jnp.zeros_like(dv)

    @pl.when(first == 1)
    def _():
        dq_ref[pl.ds(q_row, HALF), :] = jnp.zeros((HALF, dq_ref.shape[1]), dq_ref.dtype)

        def prep(head, c):
            cols = pl.ds(pl.multiple_of(head * HEAD, HEAD), HEAD)
            both = o_ref[pl.ds(q_row, HALF), cols].astype(wide) * do_ref[
                pl.ds(q_row, HALF), cols
            ].astype(wide)
            delta[pl.ds(head, 1), pl.ds(q_row, HALF)] = jnp.sum(both.T, axis=0, keepdims=True)
            return c

        lax.fori_loop(0, heads, prep, 0)

    def run(masked):
        keys = kv_ref[pl.ds(k_row, HALF), :HEAD]
        vals = kv_ref[pl.ds(k_row, HALF), HEAD:]

        def one(head):
            cols = pl.ds(pl.multiple_of(head * HEAD, HEAD), HEAD)
            rows = pl.ds(q_row, HALF)
            q = q_ref[rows, cols]
            do = do_ref[rows, cols]
            s = mm(keys, q, NT)
            p = jnp.exp2(s * scale2 - lg_ref[pl.ds(head, 1), rows])
            if masked:
                at = lax.broadcasted_iota(jnp.int32, p.shape, 0)
                p = jnp.where(at <= lax.broadcasted_iota(jnp.int32, p.shape, 1), p, 0.0)
            dp = mm(vals, do, NT)
            ds = (p * (dp - delta[pl.ds(head, 1), rows])).astype(low)
            dv[pl.ds(k_row, HALF), :] += mm(p.astype(low), do, NN)
            dk[pl.ds(k_row, HALF), :] += mm(ds, q, NN)
            dq_ref[rows, cols] += mm(ds, keys, TN)

        def body(i, c):
            for u in range(unroll):
                one(i * unroll + u)
            return c

        lax.fori_loop(0, heads // unroll, body, 0)

    @pl.when(diag == 0)
    def _():
        run(False)

    @pl.when(diag == 1)
    def _():
        run(True)

    @pl.when(step == pl.num_programs(0) - 1)
    def _():
        dkv_ref[:, :HEAD] = dk[...].astype(dkv_ref.dtype)
        dkv_ref[:, HEAD:] = dv[...].astype(dkv_ref.dtype)


def vm(n):
    return [pl.BlockSpec(memory_space=pltpu.VMEM)] * n


def attn_fwd(tab, q, kv, scale):
    rows, width = q.shape
    heads = width // HEAD
    steps = tab.shape[1]
    n = steps * heads
    return pl.pallas_call(
        functools.partial(attn_fwd_body, scale * math.log2(math.e), heads, min(8, heads)),
        out_shape=(jax.ShapeDtypeStruct((rows, width), low), jax.ShapeDtypeStruct((heads, rows), wide)),
        grid_spec=pltpu.PrefetchScalarGridSpec(
            num_scalar_prefetch=1, grid=(steps,), in_specs=vm(2), out_specs=tuple(vm(2)),
            scratch_shapes=[pltpu.VMEM((heads, HALF, 256), wide)]),
        compiler_params=pltpu.CompilerParams(dimension_semantics=("arbitrary",), vmem_limit_bytes=40 << 20),
        cost_estimate=pl.CostEstimate(flops=n * HALF * HALF * HEAD * 4, bytes_accessed=8 << 20, transcendentals=n * HALF * HALF),
    )(tab, q, kv)


def attn_bwd(tab, q, kv, o, lg, do, scale):
    rows, width = q.shape
    heads = width // HEAD
    steps = tab.shape[1]
    n = steps * heads
    return pl.pallas_call(
        functools.partial(attn_bwd_body, scale * math.log2(math.e), heads, min(4, heads)),
        out_shape=(jax.ShapeDtypeStruct((rows, width), wide), jax.ShapeDtypeStruct((kv.shape[0], 2 * HEAD), low)),
        grid_spec=pltpu.PrefetchScalarGridSpec(
            num_scalar_prefetch=1, grid=(steps,), in_specs=vm(5), out_specs=tuple(vm(2)),
            scratch_shapes=[pltpu.VMEM((kv.shape[0], HEAD), wide), pltpu.VMEM((kv.shape[0], HEAD), wide), pltpu.VMEM((heads, rows), wide)]),
        compiler_params=pltpu.CompilerParams(dimension_semantics=("arbitrary",), vmem_limit_bytes=50 << 20),
        cost_estimate=pl.CostEstimate(flops=n * HALF * HALF * HEAD * 10, bytes_accessed=16 << 20, transcendentals=n * HALF * HALF),
    )(tab, q, kv, o, lg, do)


def head_norm(x, gain):
    inv = lax.rsqrt(jnp.mean(x * x, axis=-1, keepdims=True) + epsilon)
    return x * inv * gain


def project_body(heads, x_ref, wq_ref, wkv_ref, cos_ref, sin_ref, qg_ref, kg_ref, q_ref, kv_ref, qp_ref, kp_ref):
    x = x_ref[...]
    cosine, sine = cos_ref[...], sin_ref[...]
    proj = mm(x, wq_ref[...], NN)
    qp_ref[...] = proj

    def turn(v, gain):
        n = head_norm(v, gain)
        return (n * cosine + pltpu.roll(n, HEAD // 2, 1) * sine).astype(low)

    for head in range(heads):
        cols = slice(head * HEAD, (head + 1) * HEAD)
        q_ref[:, cols] = turn(proj[:, cols], qg_ref[...])
    kv = mm(x, wkv_ref[...], NN)
    kp_ref[...] = kv[:, :HEAD]
    kv_ref[:, :HEAD] = turn(kv[:, :HEAD], kg_ref[...])
    kv_ref[:, HEAD:] = kv[:, HEAD:].astype(low)


def project(x, wq, wkv, cosine, sine, query_gain, key_gain):
    rows, depth = x.shape
    width = wq.shape[1]
    tile = 256
    by_row = lambda w: pl.BlockSpec((tile, w), lambda i: (i, 0))
    whole = lambda a: pl.BlockSpec(a.shape, lambda i: (0, 0))
    gains = (query_gain.reshape(1, HEAD), key_gain.reshape(1, HEAD))
    return pl.pallas_call(
        functools.partial(project_body, width // HEAD),
        out_shape=(
            jax.ShapeDtypeStruct((rows, width), low),
            jax.ShapeDtypeStruct((rows, 2 * HEAD), low),
            jax.ShapeDtypeStruct((rows, width), wide),
            jax.ShapeDtypeStruct((rows, HEAD), wide),
        ),
        grid=(rows // tile,),
        in_specs=[by_row(depth), whole(wq), whole(wkv), by_row(HEAD), by_row(HEAD), whole(gains[0]), whole(gains[1])],
        out_specs=(by_row(width), by_row(2 * HEAD), by_row(width), by_row(HEAD)),
        compiler_params=pltpu.CompilerParams(vmem_limit_bytes=40 << 20),
        cost_estimate=pl.CostEstimate(flops=2 * rows * depth * (width + 2 * HEAD), bytes_accessed=20 << 20, transcendentals=0),
    )(x, wq, wkv, cosine, sine, *gains)


def unproject_body(heads, scale, dz_ref, x_ref, cos_ref, sin_ref, gain_ref, gx_ref, gg_ref):
    @pl.when(pl.program_id(0) == 0)
    def _():
        gg_ref[...] = jnp.zeros_like(gg_ref)

    cosine, sine = cos_ref[...], sin_ref[...]
    terms = jnp.zeros((8, HEAD), wide)
    for head in range(heads):
        cols = slice(head * HEAD, (head + 1) * HEAD)
        gz = dz_ref[:, cols] * scale
        gz = gz * cosine - pltpu.roll(gz, HEAD // 2, 1) * sine
        x = x_ref[:, cols]
        inv = lax.rsqrt(jnp.mean(x * x, axis=-1, keepdims=True) + epsilon)
        weighted = gz * gain_ref[...]
        inner = jnp.sum(weighted * x, axis=-1, keepdims=True)
        gx_ref[:, cols] = (inv * weighted - x * (inv * inv * inv * inner / HEAD)).astype(low)
        terms += jnp.sum((gz * x * inv).reshape(-1, 8, HEAD), axis=0)
    gg_ref[...] += terms


def unproject(dz, x, cosine, sine, gain, scale):
    rows, width = x.shape
    tile = 256
    by_row = lambda w: pl.BlockSpec((tile, w), lambda i: (i, 0))
    fixed = lambda r: pl.BlockSpec((r, HEAD), lambda i: (0, 0))
    gx, gg = pl.pallas_call(
        functools.partial(unproject_body, width // HEAD, scale),
        out_shape=(jax.ShapeDtypeStruct((rows, width), low), jax.ShapeDtypeStruct((8, HEAD), wide)),
        grid=(rows // tile,),
        in_specs=[by_row(width), by_row(width), by_row(HEAD), by_row(HEAD), fixed(1)],
        out_specs=(by_row(width), fixed(8)),
        compiler_params=pltpu.CompilerParams(vmem_limit_bytes=32 << 20),
        cost_estimate=pl.CostEstimate(flops=20 * rows * width, bytes_accessed=10 * rows * width, transcendentals=0),
    )(dz, x, cosine, sine, gain.reshape(1, HEAD))
    return gx, jnp.sum(gg, axis=0)


def apply_norm(matrix, norm_gain):
    inv_rms = lax.rsqrt(jnp.mean(matrix * matrix, axis=-1, keepdims=True) + epsilon)
    return (matrix * inv_rms * norm_gain, inv_rms)


def norm_backward(matrix, inv_rms, norm_gain, gradient):
    weighted = gradient * norm_gain
    inner_sum = jnp.sum(weighted * matrix, axis=-1, keepdims=True)
    grad_matrix = (
        inv_rms * weighted - matrix * (inv_rms * inv_rms * inv_rms) * inner_sum / matrix.shape[-1]
    )
    return (grad_matrix, jnp.sum(gradient * matrix * inv_rms, axis=0))


def on_device(
    sizes,
    inputs,
    cotangent,
    stretch_ids,
    expert_ids,
    attn_gain,
    query_gain,
    key_gain,
    w_query,
    key_matrix,
    value_matrix,
    w_out,
    mlp_gain,
    w_router,
    w_gate,
    w_up,
    w_down,
):
    n_dp, n_c, n_e = sizes
    assert n_dp == 2 and w_gate.shape[0] == 1
    dp, c, z = lax.axis_index("dp"), lax.axis_index("context"), lax.axis_index("expert")
    tokens = inputs[0].astype(wide)
    tok, model = tokens.shape
    part = tok // 2
    query_heads = w_query.shape[1] // HEAD
    group = QUERY_HEADS // KEY_VALUE_HEADS
    assert query_heads <= group
    stretch = n_e * tok
    blocks = stretch_ids.shape[0]
    scale = 1.0 / math.sqrt(HEAD)
    w_gate, w_up, w_down = w_gate[0], w_up[0], w_down[0]
    flat = ("context", "expert")

    def to_peer(x, j):
        return lax.ppermute(x, "context", [(i, i ^ j) for i in range(n_c)])

    def along(x, d):
        return lax.ppermute(x, "expert", [(i, (i + d) % n_e) for i in range(n_e)])

    def across(x):
        return lax.ppermute(x, "dp", [(0, 1), (1, 0)])

    def sum_all(x):
        for name, n in (("dp", n_dp), ("context", n_c), ("expert", n_e)):
            bit = 1
            while bit < n:
                x = x + lax.ppermute(x, name, [(i, i ^ bit) for i in range(n)])
                bit *= 2
        return x

    def front(s):
        return (z - s) % n_e * tok

    def back(s):
        return (z + s) % n_e * tok + part

    def rows_of(x, s):
        return jnp.concatenate(
            [lax.dynamic_slice_in_dim(x, front(s), part, 0), lax.dynamic_slice_in_dim(x, back(s), part, 0)], axis=0
        )

    def ring(x):
        a, b = x[:part], x[part:]
        halves = [(a, b)]
        for _ in range(n_e - 1):
            a, b = along(a, 1), along(b, -1)
            halves.append((a, b))
        return halves

    def in_order(halves):
        whole = jnp.zeros((stretch, halves[0][0].shape[1]), halves[0][0].dtype)
        for s, (a, b) in enumerate(halves):
            whole = lax.dynamic_update_slice_in_dim(whole, a, front(s), 0)
            whole = lax.dynamic_update_slice_in_dim(whole, b, back(s), 0)
        return whole

    def ring_sum(term):
        a = b = None
        for s in range(n_e - 1, -1, -1):
            t = term(s)
            if a is not None:
                a, b = along(a.astype(low), -1).astype(wide), along(b.astype(low), 1).astype(wide)
                t = (t[:part] + a, t[part:] + b)
            else:
                t = (t[:part], t[part:])
            a, b = t
        return jnp.concatenate([a, b], axis=0)

    def spread(x):
        steps = []
        for a, b in ring(x):
            if n_c == 4:
                a1, b1, a2, b2 = to_peer(a, 1), to_peer(b, 1), to_peer(a, 2), to_peer(b, 2)
                pieces = [a, b, a1, b1, a2, b2, to_peer(a1, 2), to_peer(b2, 1)]
            else:
                pieces = [a, b]
                for j in range(1, n_c):
                    pieces += [to_peer(a, j), to_peer(b, j)]
            steps.append(jnp.concatenate(pieces, axis=0))
        return steps

    def collect_peers(chunk):
        a = [chunk[j * tok : j * tok + part] for j in range(n_c)]
        b = [chunk[j * tok + part : (j + 1) * tok] for j in range(n_c)]
        if n_c == 4:
            from_a, from_b = to_peer(a[3], 2), to_peer(b[3], 1)
            a1 = (a[1].astype(wide) + from_a.astype(wide)).astype(low)
            b2 = (b[2].astype(wide) + from_b.astype(wide)).astype(low)
            more_a = [to_peer(a1, 1), to_peer(a[2], 2)]
            more_b = [to_peer(b[1], 1), to_peer(b2, 2)]
        else:
            more_a = [to_peer(a[j], j) for j in range(1, n_c)]
            more_b = [to_peer(b[j], j) for j in range(1, n_c)]
        return (
            sum([t.astype(wide) for t in more_a], a[0].astype(wide)).astype(low),
            sum([t.astype(wide) for t in more_b], b[0].astype(wide)).astype(low),
        )

    def collect_line(sums):
        got_a, got_b = [sums[0][0]], [sums[0][1]]
        for s in range(1, n_e):
            got_a.append(along(sums[s][0], -s))
            got_b.append(along(sums[s][1], s))
        total = lambda parts: sum([t.astype(wide) for t in parts[1:]], parts[0].astype(wide))
        return jnp.concatenate([total(got_a), total(got_b)], axis=0)

    def reduce_pieces(matrix):
        half = matrix.shape[0] // 2
        quarter = half // n_c
        there = lax.dynamic_slice_in_dim(matrix, (1 - dp) * half, half, 0).astype(low)
        mine = lax.dynamic_slice_in_dim(matrix, dp * half, half, 0) + across(there).astype(wide)
        total = lax.dynamic_slice_in_dim(mine, c * quarter, quarter, 0)
        for j in range(1, n_c):
            piece = lax.dynamic_slice_in_dim(mine, (c ^ j) * quarter, quarter, 0)
            total = total + to_peer(piece.astype(low), j).astype(wide)
        return total.astype(low)

    def whole_rows(piece):
        quarter = piece.shape[0]
        half = quarter * n_c
        whole = jnp.zeros((2 * half, piece.shape[1]), wide)
        for j in range(n_c):
            got = to_peer(piece, j) if j else piece
            whole = lax.dynamic_update_slice_in_dim(whole, got.astype(wide), dp * half + (c ^ j) * quarter, 0)
            other = across(got)
            whole = lax.dynamic_update_slice_in_dim(
                whole, other.astype(wide), (1 - dp) * half + (c ^ j) * quarter, 0
            )
        return whole

    own_ids = lax.dynamic_slice_in_dim(stretch_ids, 2 * c, 2, 0)
    my_positions = (own_ids[:, None] * HALF + jnp.arange(HALF, dtype=jnp.int32)[None, :]).reshape(-1)
    frequency = jnp.exp(
        jnp.arange(HEAD // 2, dtype=wide) * (-2.0 * math.log(rope_base) / HEAD)
    )
    angles = my_positions.astype(wide)[:, None] * frequency[None, :]
    cosine, sine = jnp.cos(angles), jnp.sin(angles)
    cosine = jnp.concatenate([cosine, cosine], axis=1)
    sine = jnp.concatenate([-sine, sine], axis=1)
    at = jnp.arange(blocks + 1, dtype=jnp.int32)
    second = (at > own_ids[0]).astype(jnp.int32)
    key_pos = at - second * (own_ids[0] + 1)
    stored = jnp.sum(
        jnp.where(stretch_ids[None, :] == key_pos[:, None], jnp.arange(blocks, dtype=jnp.int32)[None, :], 0), axis=1
    )
    slot = ((stored // 2) ^ c) * 2 + stored % 2
    last = (key_pos == jnp.where(second == 1, own_ids[1], own_ids[0])).astype(jnp.int32)
    tab = jnp.stack([second, slot, last, (key_pos == 0).astype(jnp.int32)])

    key_first = z * query_heads // group * HEAD
    wkv = jnp.concatenate(
        [
            lax.dynamic_slice_in_dim(key_matrix, key_first, HEAD, 1),
            lax.dynamic_slice_in_dim(value_matrix, key_first, HEAD, 1),
        ],
        axis=1,
    )
    normalized, attn_inv = apply_norm(tokens, attn_gain)
    rows = in_order(ring(normalized.astype(low)))
    rows, cot = lax.optimization_barrier((rows, cotangent[0]))
    query, kv, query_proj, key_proj = project(rows, w_query, wkv, cosine, sine, query_gain, key_gain)
    kv_all = jnp.concatenate([kv] + [to_peer(kv, j) for j in range(1, n_c)], axis=0)
    attn_low, log_totals = attn_fwd(tab, query, kv_all, scale)
    branch = ring_sum(lambda s: mm(rows_of(attn_low, s), w_out, NN))
    middle = tokens + branch

    cot_steps = spread(cot)
    down_back = [mm(g, w_down, NT) for g in cot_steps]
    mlp_normed, mlp_inv = apply_norm(middle, mlp_gain)
    hidden = mlp_normed.astype(low)
    experts = w_router.shape[1]
    routes = expert_ids[0]
    logits = mm(hidden, w_router, NN)
    chosen = jnp.any(routes[:, :, None] == jnp.arange(experts, dtype=jnp.int32)[None, None, :], axis=1)
    shifted = jnp.where(chosen, logits, -jnp.inf)
    shifted = jnp.exp(shifted - jnp.max(shifted, axis=-1, keepdims=True))
    probs = shifted / jnp.sum(shifted, axis=-1, keepdims=True)
    my_probs = lax.all_to_all(probs.T, flat, 0, 0, tiled=True)
    step_at = jnp.arange(n_e, dtype=jnp.int32)[:, None, None]
    peer_at = jnp.arange(n_c, dtype=jnp.int32)[None, :, None]
    half_at = jnp.arange(2, dtype=jnp.int32)[None, None, :]
    line_at = (z + jnp.where(half_at == 0, -step_at, step_at)) % n_e
    order = (((c ^ peer_at) * n_e + line_at) * 2 + half_at).reshape(-1)
    my_probs = my_probs.reshape(-1, part)[order].reshape(n_e, n_c * tok, 1)
    hidden_steps = spread(hidden)
    gate_dots, grad_sums, kept = [], [], []
    for s in range(n_e):
        h, gd, p = hidden_steps[s], down_back[s], my_probs[s]
        if n_c != 4 and s:
            h, grad_sums[-1] = lax.optimization_barrier((h, grad_sums[-1]))
        gate_pre, up_pre = mm(h, w_gate, NN), mm(h, w_up, NN)
        sigmoid = jax.nn.sigmoid(gate_pre)
        silu = gate_pre * sigmoid
        active = silu * up_pre
        gate_dots.append(jnp.sum(active * gd, axis=-1))
        grad_active = p * gd
        grad_gate = (grad_active * up_pre * (sigmoid * (1.0 + gate_pre * (1.0 - sigmoid)))).astype(low)
        grad_up = (grad_active * silu).astype(low)
        kept.append(((p * active).astype(low), grad_gate, grad_up))
        grad_in = (mm(grad_gate, w_gate, NT) + mm(grad_up, w_up, NT)).astype(low)
        grad_sums.append(collect_peers(grad_in))
    grad_hidden = collect_line(grad_sums)
    back_order = jnp.arange(2 * n_c * n_e, dtype=jnp.int32).reshape(n_c, n_e, 2)
    c_at, z_at = jnp.arange(n_c, dtype=jnp.int32)[:, None, None], jnp.arange(n_e, dtype=jnp.int32)[None, :, None]
    back_order = ((jnp.where(half_at == 0, z - z_at, z_at - z) % n_e * n_c + (c_at ^ c)) * 2 + half_at).reshape(-1)
    dots = jnp.concatenate(gate_dots).reshape(-1, part)[back_order].reshape(experts, tok)
    grad_probs = lax.all_to_all(dots, flat, 0, 0, tiled=True).T
    grad_logits = (probs * (grad_probs - jnp.sum(probs * grad_probs, axis=-1, keepdims=True))).astype(low)
    grad_hidden = grad_hidden + mm(grad_logits, w_router, NT)
    router_part = mm(grad_logits, hidden, TN)
    grad_out = cotangent[0].astype(wide)
    grad_mid_norm, mlp_terms = norm_backward(middle, mlp_inv, mlp_gain, grad_hidden)
    grad_middle = grad_out + grad_mid_norm

    gathered = in_order(ring(grad_middle.astype(low)))
    grad_mix = mm(gathered, w_out, NT).astype(low)
    gathered, held = lax.optimization_barrier((gathered, [k[0] for k in kept]))
    out_sums = []
    for a in held:
        if n_c != 4 and out_sums:
            a, out_sums[-1] = lax.optimization_barrier((a, out_sums[-1]))
        out_sums.append(collect_peers(mm(a, w_down, NN).astype(low)))
    output = (middle + collect_line(out_sums)).astype(low)[None]
    query_grad, kv_grad = attn_bwd(tab, query, kv_all, attn_low, log_totals, grad_mix, scale)
    kv_sum = kv_grad[:stretch].astype(wide)
    for j in range(1, n_c):
        kv_sum = kv_sum + to_peer(kv_grad[j * stretch : (j + 1) * stretch], j).astype(wide)
    grad_q, query_gain_part = unproject(query_grad, query_proj, cosine, sine, query_gain, scale)
    grad_k, key_gain_part = unproject(kv_sum[:, :HEAD], key_proj, cosine, sine, key_gain, scale)
    grad_kv = jnp.concatenate([grad_k, kv_sum[:, HEAD:].astype(low)], axis=1)
    grad_normed = ring_sum(
        lambda s: mm(rows_of(grad_q, s), w_query, NT) + mm(rows_of(grad_kv, s), wkv, NT)
    )
    grad_tok_norm, attn_terms = norm_backward(tokens, attn_inv, attn_gain, grad_normed)
    grad_inputs = (grad_middle + grad_tok_norm)[None]

    def over_dp(left, right, dim):
        total = sum([mm(a, b, TN) for a, b in zip(left, right)])
        half = total.shape[dim] // 2
        there = lax.dynamic_slice_in_dim(total, (1 - dp) * half, half, dim).astype(low)
        return (lax.dynamic_slice_in_dim(total, dp * half, half, dim) + across(there).astype(wide))[None]

    grad_w_gate = over_dp(hidden_steps, [k[1] for k in kept], 0)
    grad_w_up = over_dp(hidden_steps, [k[2] for k in kept], 0)
    grad_w_down = over_dp([k[0] for k in kept], cot_steps, 1)
    grad_w_out = whole_rows(reduce_pieces(mm(attn_low, gathered, TN)))
    grad_w_query = whole_rows(reduce_pieces(mm(rows, grad_q, TN)))
    kv_piece = reduce_pieces(mm(rows, grad_kv, TN))
    every = jnp.zeros((n_e,) + kv_piece.shape, low)
    for d in range(n_e):
        every = lax.dynamic_update_slice_in_dim(every, (along(kv_piece, d) if d else kv_piece)[None], (z - d) % n_e, 0)
    every = every.reshape(KEY_VALUE_HEADS, -1, kv_piece.shape[0], 2, HEAD).astype(wide).sum(1)
    every = every.transpose(1, 2, 0, 3).reshape(kv_piece.shape[0], 2 * KEY_VALUE_HEADS * HEAD)
    grad_w_kv = whole_rows(every.astype(low))
    kv_width = KEY_VALUE_HEADS * HEAD

    early = sum_all(jnp.concatenate([router_part, mlp_terms[None]], axis=0))
    gains = jnp.concatenate([query_gain_part, key_gain_part, jnp.zeros((model - 2 * HEAD,), wide)])
    late = sum_all(jnp.stack([attn_terms, gains]))
    return (
        output,
        grad_inputs,
        late[0],
        late[1, :HEAD],
        late[1, HEAD : 2 * HEAD],
        grad_w_query,
        grad_w_kv[:, :kv_width],
        grad_w_kv[:, kv_width:],
        grad_w_out,
        early[experts],
        early[:experts].T,
        grad_w_gate,
        grad_w_up,
        grad_w_down,
    )


def solution(mesh):
    across_all = P("dp", ("context", "expert"), None)
    experts = P(("context", "expert"), None, None)
    in_specs = (
        across_all,
        across_all,
        P(),
        across_all,
        P(),
        P(),
        P(),
        P(None, "expert"),
        P(),
        P(),
        P("expert", None),
        P(),
        P(),
        experts,
        experts,
        experts,
    )
    out_specs = (
        across_all,
        across_all,
        P(),
        P(),
        P(),
        P(None, "expert"),
        P(),
        P(),
        P("expert", None),
        P(),
        P(),
        P(("context", "expert"), "dp", None),
        P(("context", "expert"), "dp", None),
        P(("context", "expert"), None, "dp"),
    )
    sizes = (mesh.shape["dp"], mesh.shape["context"], mesh.shape["expert"])
    return jax.shard_map(
        functools.partial(on_device, sizes), mesh=mesh, in_specs=in_specs, out_specs=out_specs, check_vma=False
    )
```
